256 devices in a mesh: plane: 16 (over x, z_lo, core), tm: 16 (over y, z_hi).
Axes of the slice: x: 4, y: 4, z: 8 (z_hi: 4, z_lo: 2; z = z_hi * 2 + z_lo), core: 2. Of those that a mesh axis runs over, the one named last changes fastest.
Arguments:
- coeffs: float32 [64, 3, 16, 2048], P('tm', None, None, 'plane'), may hold values from -1.5 to 1.5
- radius: float32 [2048], P('plane'), may hold values from 0.25 to 2
- tile_mask: int32 [4, 16, 1], P(None, 'plane'), may hold values from 0 to 1
Outputs:
- hazard: float32 [4, 2048], P(None, 'plane')
The draws below stay inside these ranges and needn't reach their ends.
All inputs are finite; a program needn't handle non-finite values.
Results may differ from the reference program's by a relative error of at most 0.0003.
Values sent between devices are 32-bit elements; how exact they have to be, the bound alone decides.
A program may use at most 64 MiB of HBM per device.

```python
import math
import jax
import jax.numpy as jnp
from jax import lax

OBJ = 128
SAMP = 32
K = 16
TILE = 128
ROUNDS = 4
WINDOWS = 64
OBJECTS = 2048


def draw_tile_mask(key, part):
    blocks = OBJECTS // OBJ
    tile_count = OBJ // TILE
    first_key, second_key = jax.random.split(jax.random.fold_in(key, 11))
    density = jax.random.randint(first_key, (blocks,), 1, 10)
    row_density = jnp.repeat(density, tile_count)
    scores = jax.random.randint(second_key, (ROUNDS, OBJECTS // TILE, tile_count), 0, 10)
    return (scores < row_density[None, :, None]).astype(jnp.int32)


def level_of(stream_key, dims, cuts, least, largest):
    gain = 1.0
    for dim, blocks in cuts:
        heights = jax.random.uniform(jax.random.fold_in(jax.random.fold_in(stream_key, 6), dim), (blocks,), jnp.float32, least / len(cuts), largest / len(cuts))
        gain = gain * jnp.repeat(jnp.exp(heights), dims[dim] // blocks).reshape((-1,) + (1,) * (len(dims) - 1 - dim))
    return gain


def scatter_about(key, shape, deviation, most, cuts=(), kind=jnp.bfloat16):
    entries = deviation * jax.random.normal(key, shape, jnp.float32)
    if cuts:
        entries = entries * level_of(key, shape, cuts, -0.22, 0.18)
    return jnp.clip(entries, -most, most).astype(kind)


def setup_inputs(seed: int = 0) -> dict:
    key_of = jax.random.split(jax.random.key(seed), 4)
    return {
        "coeffs": scatter_about(key_of[0], (WINDOWS, 3, K, OBJECTS), 0.25, 1.5, ((0, 16), (3, 16)), jnp.float32),
        "radius": jnp.clip(jnp.exp(math.log(2.0) - 2.0794415 * jax.random.uniform(key_of[1], (OBJECTS,), jnp.float32) ** level_of(key_of[1], (OBJECTS,), ((0, 16),), -0.2, 0.2)), 0.25, 2.0),
        "tile_mask": draw_tile_mask(jax.random.fold_in(key_of[3], 71), 0),
    }


def basis_table(degrees):
    sample = jnp.arange(SAMP, dtype=jnp.float32)
    nodes = -1.0 + (2.0 * sample + 1.0) / SAMP
    series = [jnp.ones_like(nodes), nodes]
    for degree in range(2, degrees):
        series.append(2.0 * nodes * series[-1] - series[-2])
    return jnp.stack(series[:degrees], axis=1)


def synthesize(basis, coeff_block):
    return jnp.einsum("sk,wckn->wcsn", basis, coeff_block, precision=lax.Precision.HIGHEST)


def pair_tile(own_slice, far_slice, own_radius, far_radius):
    inverse = 1.0 / (own_radius[:, None] + far_radius[None, :])
    separation = own_slice[:, :, :, :, None] - far_slice[:, :, :, None, :]
    squared = jnp.sum(separation * separation, axis=1)
    return jnp.sum(jnp.exp(-squared * inverse), axis=(0, 1, 3))


def reference(coeffs, radius, tile_mask):
    basis = basis_table(K)
    positions = synthesize(basis, coeffs)
    groups = OBJECTS // OBJ
    tile_count = OBJ // TILE
    normalizer = 1.0 / (WINDOWS * SAMP * TILE)
    round_rows = []
    for round_no in range(ROUNDS):
        offset = (round_no // 2 + 1) * (1 if round_no % 2 == 0 else -1)

        def block_round(block):
            partner = (block - offset) % groups
            own_pos = lax.dynamic_slice_in_dim(positions, (block * OBJ).astype(jnp.int32), OBJ, 3)
            far_pos = lax.dynamic_slice_in_dim(positions, (partner * OBJ).astype(jnp.int32), OBJ, 3)
            own_rad = lax.dynamic_slice_in_dim(radius, (block * OBJ).astype(jnp.int32), OBJ, 0)
            far_rad = lax.dynamic_slice_in_dim(radius, (partner * OBJ).astype(jnp.int32), OBJ, 0)
            mask_rows = lax.dynamic_slice_in_dim(tile_mask[round_no], (block * tile_count).astype(jnp.int32), tile_count, 0)
            pieces = []
            for own_tile in range(tile_count):
                running = jnp.zeros((TILE,), jnp.float32)
                for far_tile in range(tile_count):
                    value = pair_tile(own_pos[:, :, :, own_tile * TILE:(own_tile + 1) * TILE],
                                      far_pos[:, :, :, far_tile * TILE:(far_tile + 1) * TILE],
                                      own_rad[own_tile * TILE:(own_tile + 1) * TILE],
                                      far_rad[far_tile * TILE:(far_tile + 1) * TILE])
                    running = running + jnp.where(mask_rows[own_tile, far_tile] > 0, value, jnp.zeros_like(value))
                pieces.append(running)
            return jnp.concatenate(pieces)

        per_block = lax.map(block_round, jnp.arange(groups, dtype=jnp.int32))
        round_rows.append(per_block.reshape(OBJECTS) * normalizer)
    return jnp.stack(round_rows)
```

```python
import functools

import jax
import jax.numpy as jnp
from jax import lax
from jax.experimental import pallas as pl
from jax.experimental.pallas import tpu as pltpu
from jax.sharding import Mesh
from jax.sharding import PartitionSpec as P

SAMP = 32
TILE = 128
ROUNDS = 4
K = 16
WIN = 4
FEATS = 24
SUB = 8
LOG2E = 1.4426950408889634
TM = ("tm_0", "tm_1")
MESH = pl.DeviceIdType.MESH
f32 = jnp.float32
bf16 = jnp.bfloat16


def split3(x):
    h = x.astype(bf16).astype(f32)
    rest = x - h
    m = rest.astype(bf16).astype(f32)
    return h, m, rest - m


def basis_parts():
    shape = (SAMP, 5 * K)
    sample = lax.broadcasted_iota(jnp.int32, shape, 0).astype(f32)
    lane = lax.broadcasted_iota(jnp.int32, shape, 1)
    degree = lane % K
    t = -1.0 + (2.0 * sample + 1.0) / SAMP
    before, now = jnp.ones_like(t), t
    table = jnp.where(degree == 0, before, now)
    for k in range(2, K):
        before, now = now, 2.0 * t * now - before
        table = jnp.where(degree == k, now, table)
    h, m, l = split3(table)
    part = lane // K
    return jnp.where(part == 4, l, jnp.where(part == 2, m, h)).astype(bf16)


def positions(basis, coef):
    n = coef.shape[1]
    h, m, l = split3(coef)
    columns = []
    for c in range(3):
        rows = slice(K * c, K * c + K)
        columns.append(jnp.concatenate([h[rows], m[rows], h[rows], l[rows], h[rows]], axis=0).astype(bf16))
    pos = jnp.dot(basis, jnp.concatenate(columns, axis=1), preferred_element_type=f32)
    return [pos[:, c * n : (c + 1) * n] for c in range(3)]


def features(pos, own):
    parts = [split3(p) for p in pos]
    norm = pos[0] * pos[0] + pos[1] * pos[1] + pos[2] * pos[2]
    norms = list(split3(norm))
    ones = [jnp.ones_like(norm)] * 3
    if own:
        return [-2.0 * parts[c][r] for r in (0, 0, 1, 0, 2, 1) for c in range(3)] + ones + norms
    return [parts[c][r] for r in (0, 1, 0, 2, 0, 1) for c in range(3)] + norms + ones


def stacked(feats, b):
    return jnp.concatenate([f[SUB * b : SUB * b + SUB] for f in feats], axis=0)


def kernel(
    coef, rad, mask, out,
    own, own_rad, own_mask, far, far_rad, lhs, mean, scale, acc, part_r, part_c, mine, step1, step1_c, step2,
    load_sem, send_sem, recv_sem, rad_send, rad_recv, r_send, r_recv, c_send, c_recv, y_send, y_recv,
):
    planes = lax.axis_size("plane")
    g = lax.axis_index("plane")
    y = lax.axis_index("tm_0")
    z = lax.axis_index("tm_1")

    def plane(step):
        return lax.rem(g + step + planes, planes)

    def other(i, step):
        return lax.rem(i + step, 4)

    barrier = pltpu.get_barrier_semaphore()

    def greet(device):
        pl.semaphore_signal(barrier, inc=1, device_id=device, device_id_type=MESH)

    for d in (1, 2):
        greet((plane(-d), y, z))
        for k in range(4):
            greet((plane(d), y, other(z, k)))
    for k in (1, 2, 3):
        greet((g, y, other(z, k)))
        greet((g, other(y, k), z))

    loads = [
        pltpu.make_async_copy(coef, own, load_sem.at[0]),
        pltpu.make_async_copy(rad, own_rad, load_sem.at[1]),
        pltpu.make_async_copy(mask, own_mask, load_sem.at[2]),
    ]
    for copy in loads:
        copy.start()
    basis = basis_parts()

    pl.semaphore_wait(barrier, 16)

    def coef_copy(w, d):
        return pltpu.make_async_remote_copy(
            src_ref=coef.at[w], dst_ref=far.at[d, w], send_sem=send_sem.at[d, w], recv_sem=recv_sem.at[d, w],
            device_id=(plane(d + 1), y, z), device_id_type=MESH,
        )

    def rad_copy(d):
        return pltpu.make_async_remote_copy(
            src_ref=rad, dst_ref=far_rad.at[d], send_sem=rad_send.at[d], recv_sem=rad_recv.at[d],
            device_id=(plane(d + 1), y, z), device_id_type=MESH,
        )

    for d in range(2):
        rad_copy(d).start()
    for w in range(WIN):
        for d in range(2):
            coef_copy(w, d).start()

    for copy in loads:
        copy.wait()

    def prepare(w, carry):
        c = own[w]
        mu = jnp.mean(c, axis=1, keepdims=True)
        mean[w] = jnp.broadcast_to(mu, c.shape)
        feats = features(positions(basis, c - mu), True)
        for b in range(SAMP // SUB):
            lhs[w, b] = stacked(feats, b).T.astype(bf16)
        return carry

    lax.fori_loop(0, WIN, prepare, 0)

    for d in range(2):
        rad_copy(d).wait_recv()
    column = jnp.broadcast_to(own_rad[...], (TILE, TILE)).T
    for d in range(2):
        scale[:, TILE * d : TILE * d + TILE] = -LOG2E / (column + far_rad[d])
    acc[...] = jnp.zeros_like(acc)

    rows = 32
    turn = lax.broadcasted_iota(jnp.int32, (rows, FEATS * SUB), 1) % SUB

    def window(w, carry):
        for d in range(2):
            coef_copy(w, d).wait_recv()
        mu = mean[w]
        c = jnp.concatenate([far[0, w] - mu, far[1, w] - mu], axis=1)
        feats = features(positions(basis, c), False)
        for b in range(SAMP // SUB):
            rhs = stacked(feats, b).astype(bf16)
            for i in range(TILE // rows):
                here = slice(rows * i, rows * i + rows)
                left = lhs[w, b, here, :]
                zero = jnp.zeros_like(left)
                big = jnp.concatenate([jnp.where(turn == s, left, zero) for s in range(SUB)], axis=0)
                dist = jnp.dot(big, rhs, preferred_element_type=f32)
                sc = scale[here, :]
                total = None
                for s in range(SUB):
                    term = jnp.exp2(dist[rows * s : rows * s + rows] * sc)
                    total = term if total is None else total + term
                acc[here, :] += total
        return carry

    lax.fori_loop(0, WIN, window, 0)

    sums = acc[...]
    part_r[0:1, :] = jnp.sum(sums[:, :TILE].T, axis=0, keepdims=True)
    part_r[1:2, :] = jnp.sum(sums[:, TILE:].T, axis=0, keepdims=True)
    column_sums = jnp.sum(sums, axis=0, keepdims=True)
    for d in range(2):
        part_c[d] = column_sums[:, TILE * d : TILE * d + TILE]

    def row_copy(k, slot):
        return pltpu.make_async_remote_copy(
            src_ref=part_r, dst_ref=step1.at[slot], send_sem=r_send.at[k], recv_sem=r_recv.at[slot],
            device_id=(g, y, other(z, k)), device_id_type=MESH,
        )

    def column_copy(d, k, slot):
        return pltpu.make_async_remote_copy(
            src_ref=part_c.at[d], dst_ref=step1_c.at[d, slot], send_sem=c_send.at[d, k], recv_sem=c_recv.at[d, slot],
            device_id=(plane(-d - 1), y, other(z, k)), device_id_type=MESH,
        )

    for k in range(4):
        for d in range(2):
            column_copy(d, k, z).start()
        if k:
            row_copy(k, z).start()
    step1[z] = part_r[...]
    for k in range(4):
        if k:
            row_copy(k, other(z, k)).wait_recv()
        for d in range(2):
            column_copy(d, k, other(z, k)).wait_recv()
    mine[0:2, :] = (step1[0] + step1[1]) + (step1[2] + step1[3])
    for d in range(2):
        mine[2 + d : 3 + d, :] = (step1_c[d, 0] + step1_c[d, 1]) + (step1_c[d, 2] + step1_c[d, 3])

    def y_copy(k, slot):
        return pltpu.make_async_remote_copy(
            src_ref=mine, dst_ref=step2.at[slot], send_sem=y_send.at[k], recv_sem=y_recv.at[slot],
            device_id=(g, other(y, k), z), device_id_type=MESH,
        )

    for k in (1, 2, 3):
        y_copy(k, y).start()
    step2[y] = mine[...]
    for k in (1, 2, 3):
        y_copy(k, other(y, k)).wait_recv()
    total = (step2[0] + step2[1]) + (step2[2] + step2[3])
    for d in range(2):
        for row, r in ((d, 2 * d), (2 + d, 2 * d + 1)):
            line = total[row : row + 1, :]
            out[r : r + 1, :] = jnp.where(own_mask[0, r] > 0, line, jnp.zeros_like(line))

    for d in range(2):
        rad_copy(d).wait_send()
        for w in range(WIN):
            coef_copy(w, d).wait_send()
    for k in range(4):
        for d in range(2):
            column_copy(d, k, z).wait_send()
        if k:
            row_copy(k, z).wait_send()
            y_copy(k, y).wait_send()


def local(coeffs, radius, tile_mask):
    vmem = pltpu.VMEM
    dma = pltpu.SemaphoreType.DMA
    sums = pl.pallas_call(
        kernel,
        out_shape=jax.ShapeDtypeStruct((4, TILE), f32),
        in_specs=[pl.BlockSpec(memory_space=pltpu.HBM)] * 3,
        out_specs=pl.BlockSpec(memory_space=pltpu.VMEM),
        scratch_shapes=[
            vmem((WIN, 3 * K, TILE), f32),
            vmem((1, TILE), f32),
            pltpu.SMEM((1, ROUNDS), jnp.int32),
            vmem((2, WIN, 3 * K, TILE), f32),
            vmem((2, 1, TILE), f32),
            vmem((WIN, SAMP // SUB, TILE, FEATS * SUB), bf16),
            vmem((WIN, 3 * K, TILE), f32),
            vmem((TILE, 2 * TILE), f32),
            vmem((TILE, 2 * TILE), f32),
            vmem((2, TILE), f32),
            vmem((2, 1, TILE), f32),
            vmem((4, TILE), f32),
            vmem((4, 2, TILE), f32),
            vmem((2, 4, 1, TILE), f32),
            vmem((4, 4, TILE), f32),
            dma((3,)),
            dma((2, WIN)),
            dma((2, WIN)),
            dma((2,)),
            dma((2,)),
            dma((4,)),
            dma((4,)),
            dma((2, 4)),
            dma((2, 4)),
            dma((4,)),
            dma((4,)),
        ],
        compiler_params=pltpu.CompilerParams(
            collective_id=0, has_side_effects=True, vmem_limit_bytes=32 << 20
        ),
    )(*[pltpu.with_memory_space_constraint(x, pltpu.HBM) for x in (coeffs.reshape(WIN, 3 * K, TILE), radius.reshape(1, TILE), tile_mask.reshape(1, ROUNDS))])
    time_count = lax.axis_size(TM)
    normalizer = 1.0 / (coeffs.shape[0] * time_count * SAMP * TILE)
    return sums * normalizer


def solution(mesh):
    torus = Mesh(mesh.devices.reshape(mesh.shape["plane"], 4, 4), ("plane", "tm_0", "tm_1"))
    in_specs = (P(TM, None, None, "plane"), P("plane"), P(None, "plane", None))
    out_specs = P(None, "plane")
    return jax.shard_map(local, mesh=torus, in_specs=in_specs, out_specs=out_specs, check_vma=False)
```

```python
import jax
import jax.numpy as jnp
from jax import lax
from jax.experimental import pallas as pl
from jax.experimental.pallas import tpu as pltpu
from jax.sharding import Mesh
from jax.sharding import PartitionSpec as P

SAMP = 32
TILE = 128
ROUNDS = 4
K = 16
WIN = 4
FEATS = 24
SUB = 8
LOG2E = 1.4426950408889634
TM = ("tm_0", "tm_1")
FAR_FIRST = sorted(
    ((a, k) for a in range(4) for k in range(4)), key=lambda s: -(min(s[0], 4 - s[0]) + 2 * min(s[1], 4 - s[1]))
)
MESH = pl.DeviceIdType.MESH
f32 = jnp.float32
bf16 = jnp.bfloat16


def split3(x):
    h = x.astype(bf16).astype(f32)
    rest = x - h
    m = rest.astype(bf16).astype(f32)
    return h, m, rest - m


def basis_parts():
    shape = (SAMP, 5 * K)
    sample = lax.broadcasted_iota(jnp.int32, shape, 0).astype(f32)
    lane = lax.broadcasted_iota(jnp.int32, shape, 1)
    degree = lane % K
    t = -1.0 + (2.0 * sample + 1.0) / SAMP
    before, now = jnp.ones_like(t), t
    table = jnp.where(degree == 0, before, now)
    for k in range(2, K):
        before, now = now, 2.0 * t * now - before
        table = jnp.where(degree == k, now, table)
    h, m, l = split3(table)
    part = lane // K
    return jnp.where(part == 4, l, jnp.where(part == 2, m, h)).astype(bf16)


def positions(basis, coef):
    n = coef.shape[1]
    h, m, l = split3(coef)
    columns = []
    for c in range(3):
        rows = slice(K * c, K * c + K)
        columns.append(jnp.concatenate([h[rows], m[rows], h[rows], l[rows], h[rows]], axis=0).astype(bf16))
    pos = jnp.dot(basis, jnp.concatenate(columns, axis=1), preferred_element_type=f32)
    return [pos[:, c * n : (c + 1) * n] for c in range(3)]


def features(pos, own):
    parts = [split3(p) for p in pos]
    norm = pos[0] * pos[0] + pos[1] * pos[1] + pos[2] * pos[2]
    norms = list(split3(norm))
    ones = [jnp.ones_like(norm)] * 3
    if own:
        return [-2.0 * parts[c][r] for r in (0, 0, 1, 0, 2, 1) for c in range(3)] + ones + norms
    return [parts[c][r] for r in (0, 1, 0, 2, 0, 1) for c in range(3)] + norms + ones


def stacked(feats, b):
    return jnp.concatenate([f[SUB * b : SUB * b + SUB] for f in feats], axis=0)


def kernel(
    coef, rad, mask, out,
    own, own_rad, own_mask, far, far_rad, lhs, mean, scale, acc, part_r, part_c, all_r, all_c,
    load_sem, send_sem, recv_sem, rad_send, rad_recv, r_send, r_recv, c_send, c_recv, known_z, known_plane,
):
    planes = lax.axis_size("plane")
    g = lax.axis_index("plane")
    y = lax.axis_index("tm_0")
    z = lax.axis_index("tm_1")

    def plane(step):
        return lax.rem(g + step + planes, planes)

    def other(i, step):
        return lax.rem(i + step, 4)

    barrier = pltpu.get_barrier_semaphore()

    def greet(device):
        pl.semaphore_signal(barrier, inc=1, device_id=device, device_id_type=MESH)

    for d in (1, 2):
        greet((plane(-d), y, z))
    for k in (2, 1, 3):
        greet((g, y, other(z, k)))
        greet((g, other(y, k), z))

    loads = [
        pltpu.make_async_copy(coef, own, load_sem.at[0]),
        pltpu.make_async_copy(rad, own_rad, load_sem.at[1]),
        pltpu.make_async_copy(mask, own_mask, load_sem.at[2]),
    ]
    for copy in loads:
        copy.start()
    basis = basis_parts()

    pl.semaphore_wait(barrier, 8)
    for k in (2, 1, 3):
        pl.semaphore_signal(known_z, inc=1, device_id=(g, y, other(z, k)), device_id_type=MESH)

    def coef_copy(w, d):
        return pltpu.make_async_remote_copy(
            src_ref=coef.at[w], dst_ref=far.at[d, w], send_sem=send_sem.at[d, w], recv_sem=recv_sem.at[d, w],
            device_id=(plane(d + 1), y, z), device_id_type=MESH,
        )

    def rad_copy(d):
        return pltpu.make_async_remote_copy(
            src_ref=rad, dst_ref=far_rad.at[d], send_sem=rad_send.at[d], recv_sem=rad_recv.at[d],
            device_id=(plane(d + 1), y, z), device_id_type=MESH,
        )

    for d in range(2):
        rad_copy(d).start()
    for w in range(WIN):
        for d in range(2):
            coef_copy(w, d).start()

    for copy in loads:
        copy.wait()

    def prepare(w, carry):
        c = own[w]
        mu = jnp.mean(c, axis=1, keepdims=True)
        mean[w] = jnp.broadcast_to(mu, c.shape)
        feats = features(positions(basis, c - mu), True)
        for b in range(SAMP // SUB):
            lhs[w, b] = stacked(feats, b).T.astype(bf16)
        return carry

    lax.fori_loop(0, WIN, prepare, 0)

    for d in range(2):
        rad_copy(d).wait_recv()
    column = jnp.broadcast_to(own_rad[...], (TILE, TILE)).T
    for d in range(2):
        scale[:, TILE * d : TILE * d + TILE] = -LOG2E / (column + far_rad[d])
    acc[...] = jnp.zeros_like(acc)

    rows = 32
    turn = lax.broadcasted_iota(jnp.int32, (rows, FEATS * SUB), 1) % SUB

    def window(w, carry):
        for d in range(2):
            coef_copy(w, d).wait_recv()
        mu = mean[w]
        c = jnp.concatenate([far[0, w] - mu, far[1, w] - mu], axis=1)
        feats = features(positions(basis, c), False)
        for b in range(SAMP // SUB):
            rhs = stacked(feats, b).astype(bf16)
            for i in range(TILE // rows):
                here = slice(rows * i, rows * i + rows)
                left = lhs[w, b, here, :]
                zero = jnp.zeros_like(left)
                big = jnp.concatenate([jnp.where(turn == s, left, zero) for s in range(SUB)], axis=0)
                dist = jnp.dot(big, rhs, preferred_element_type=f32)
                sc = scale[here, :]
                total = None
                for s in range(SUB):
                    term = jnp.exp2(dist[rows * s : rows * s + rows] * sc)
                    total = term if total is None else total + term
                acc[here, :] += total
        return carry

    lax.fori_loop(0, WIN // 2, window, 0)
    pl.semaphore_wait(known_z, 3)
    for d in (1, 2):
        pl.semaphore_signal(known_plane, inc=1, device_id=(plane(d), y, z), device_id_type=MESH)
    lax.fori_loop(WIN // 2, WIN, window, 0)

    sums = acc[...]
    part_r[0:1, :] = jnp.sum(sums[:, :TILE].T, axis=0, keepdims=True)
    part_r[1:2, :] = jnp.sum(sums[:, TILE:].T, axis=0, keepdims=True)
    column_sums = jnp.sum(sums, axis=0, keepdims=True)
    for d in range(2):
        part_c[d] = column_sums[:, TILE * d : TILE * d + TILE]

    def row_copy(a, k, ys, zs):
        slot = 4 * ys + zs
        return pltpu.make_async_remote_copy(
            src_ref=part_r, dst_ref=all_r.at[slot], send_sem=r_send.at[a, k], recv_sem=r_recv.at[slot],
            device_id=(g, other(y, a), other(z, k)), device_id_type=MESH,
        )

    def column_copy(d, a, k, ys, zs):
        slot = 4 * ys + zs
        return pltpu.make_async_remote_copy(
            src_ref=part_c.at[d], dst_ref=all_c.at[d, slot], send_sem=c_send.at[d, a, k], recv_sem=c_recv.at[d, slot],
            device_id=(plane(-d - 1), other(y, a), other(z, k)), device_id_type=MESH,
        )

    pl.semaphore_wait(known_plane, 2)
    for a, k in FAR_FIRST:
        for d in range(2):
            column_copy(d, a, k, y, z).start()
        if a or k:
            row_copy(a, k, y, z).start()
    all_r[4 * y + z] = part_r[...]

    for d in range(2):
        rad_copy(d).wait_send()
        for w in range(WIN):
            coef_copy(w, d).wait_send()
    for a, k in reversed(FAR_FIRST):
        for d in range(2):
            column_copy(d, a, k, y, z).wait_send()
        if a or k:
            row_copy(a, k, y, z).wait_send()

    for a, k in reversed(FAR_FIRST):
        if a or k:
            row_copy(a, k, other(y, a), other(z, k)).wait_recv()
        for d in range(2):
            column_copy(d, a, k, other(y, a), other(z, k)).wait_recv()
    rows_total = jnp.sum(all_r[...], axis=0)
    for d in range(2):
        for r, line in ((2 * d, rows_total[d : d + 1, :]), (2 * d + 1, jnp.sum(all_c[d], axis=0))):
            out[r : r + 1, :] = jnp.where(own_mask[0, r] > 0, line, jnp.zeros_like(line))


def local(coeffs, radius, tile_mask):
    vmem = pltpu.VMEM
    dma = pltpu.SemaphoreType.DMA
    sums = pl.pallas_call(
        kernel,
        out_shape=jax.ShapeDtypeStruct((4, TILE), f32),
        in_specs=[pl.BlockSpec(memory_space=pltpu.HBM)] * 3,
        out_specs=pl.BlockSpec(memory_space=pltpu.VMEM),
        scratch_shapes=[
            vmem((WIN, 3 * K, TILE), f32),
            vmem((1, TILE), f32),
            pltpu.SMEM((1, ROUNDS), jnp.int32),
            vmem((2, WIN, 3 * K, TILE), f32),
            vmem((2, 1, TILE), f32),
            vmem((WIN, SAMP // SUB, TILE, FEATS * SUB), bf16),
            vmem((WIN, 3 * K, TILE), f32),
            vmem((TILE, 2 * TILE), f32),
            vmem((TILE, 2 * TILE), f32),
            vmem((2, TILE), f32),
            vmem((2, 1, TILE), f32),
            vmem((16, 2, TILE), f32),
            vmem((2, 16, 1, TILE), f32),
            dma((3,)),
            dma((2, WIN)),
            dma((2, WIN)),
            dma((2,)),
            dma((2,)),
            dma((4, 4)),
            dma((16,)),
            dma((2, 4, 4)),
            dma((2, 16)),
            pltpu.SemaphoreType.REGULAR,
            pltpu.SemaphoreType.REGULAR,
        ],
        compiler_params=pltpu.CompilerParams(
            collective_id=0, has_side_effects=True, vmem_limit_bytes=32 << 20
        ),
    )(*[pltpu.with_memory_space_constraint(x, pltpu.HBM) for x in (coeffs.reshape(WIN, 3 * K, TILE), radius.reshape(1, TILE), tile_mask.reshape(1, ROUNDS))])
    time_count = lax.axis_size(TM)
    normalizer = 1.0 / (coeffs.shape[0] * time_count * SAMP * TILE)
    return sums * normalizer


def solution(mesh):
    torus = Mesh(mesh.devices.reshape(mesh.shape["plane"], 4, 4), ("plane", "tm_0", "tm_1"))
    in_specs = (P(TM, None, None, "plane"), P("plane"), P(None, "plane", None))
    out_specs = P(None, "plane")
    return jax.shard_map(local, mesh=torus, in_specs=in_specs, out_specs=out_specs, check_vma=False)
```

```python
import jax
import jax.numpy as jnp
from jax import lax
from jax.experimental import pallas as pl
from jax.experimental.pallas import tpu as pltpu
from jax.sharding import Mesh
from jax.sharding import PartitionSpec as P

SAMP = 32
TILE = 128
ROUNDS = 4
K = 16
WIN = 4
FEATS = 24
SUB = 8
LOG2E = 1.4426950408889634
TM = ("tm_0", "tm_1")
FAR_FIRST = sorted(
    ((a, k) for a in range(4) for k in range(4)), key=lambda s: -(min(s[0], 4 - s[0]) + 2 * min(s[1], 4 - s[1]))
)
MESH = pl.DeviceIdType.MESH
f32 = jnp.float32
bf16 = jnp.bfloat16


def split3(x):
    h = x.astype(bf16).astype(f32)
    rest = x - h
    m = rest.astype(bf16).astype(f32)
    return h, m, rest - m


def basis_parts():
    shape = (SAMP, 5 * K)
    sample = lax.broadcasted_iota(jnp.int32, shape, 0).astype(f32)
    lane = lax.broadcasted_iota(jnp.int32, shape, 1)
    degree = lane % K
    t = -1.0 + (2.0 * sample + 1.0) / SAMP
    before, now = jnp.ones_like(t), t
    table = jnp.where(degree == 0, before, now)
    for k in range(2, K):
        before, now = now, 2.0 * t * now - before
        table = jnp.where(degree == k, now, table)
    h, m, l = split3(table)
    part = lane // K
    return jnp.where(part == 4, l, jnp.where(part == 2, m, h)).astype(bf16)


def positions(basis, coef):
    n = coef.shape[1]
    h, m, l = split3(coef)
    columns = []
    for c in range(3):
        rows = slice(K * c, K * c + K)
        columns.append(jnp.concatenate([h[rows], m[rows], h[rows], l[rows], h[rows]], axis=0).astype(bf16))
    pos = jnp.dot(basis, jnp.concatenate(columns, axis=1), preferred_element_type=f32)
    return [pos[:, c * n : (c + 1) * n] for c in range(3)]


def features(pos, own):
    parts = [split3(p) for p in pos]
    norm = pos[0] * pos[0] + pos[1] * pos[1] + pos[2] * pos[2]
    norms = list(split3(norm))
    ones = [jnp.ones_like(norm)] * 3
    if own:
        return [-2.0 * parts[c][r] for r in (0, 0, 1, 0, 2, 1) for c in range(3)] + ones + norms
    return [parts[c][r] for r in (0, 1, 0, 2, 0, 1) for c in range(3)] + norms + ones


def stacked(feats, b):
    return jnp.concatenate([f[SUB * b : SUB * b + SUB] for f in feats], axis=0)


def kernel(
    coef, rad, mask, out,
    own, own_rad, own_mask, far, far_rad, lhs, mean, scale, acc, part_r, part_c, all_r, all_c,
    load_sem, send_sem, recv_sem, rad_send, rad_recv, r_send, r_recv, c_send, c_recv, known,
):
    planes = lax.axis_size("plane")
    g = lax.axis_index("plane")
    y = lax.axis_index("tm_0")
    z = lax.axis_index("tm_1")

    def plane(step):
        return lax.rem(g + step + planes, planes)

    def other(i, step):
        return lax.rem(i + step, 4)

    barrier = pltpu.get_barrier_semaphore()

    def greet(device):
        pl.semaphore_signal(barrier, inc=1, device_id=device, device_id_type=MESH)

    for d in (1, 2):
        greet((plane(-d), y, z))
    for k in (1, 3):
        greet((g, y, other(z, k)))
    for k in (2, 1, 3):
        greet((g, other(y, k), z))

    loads = [
        pltpu.make_async_copy(coef, own, load_sem.at[0]),
        pltpu.make_async_copy(rad, own_rad, load_sem.at[1]),
        pltpu.make_async_copy(mask, own_mask, load_sem.at[2]),
    ]
    for copy in loads:
        copy.start()
    basis = basis_parts()

    pl.semaphore_wait(barrier, 7)

    def tell(turn, devices):
        for device in devices:
            pl.semaphore_signal(known.at[turn], inc=1, device_id=device, device_id_type=MESH)

    next_z = [(g, y, other(z, k)) for k in (1, 3)]
    next_plane = [(plane(d), y, z) for d in (1, 2)]
    tell(0, next_z)

    def coef_copy(w, d):
        return pltpu.make_async_remote_copy(
            src_ref=coef.at[w], dst_ref=far.at[d, w], send_sem=send_sem.at[d, w], recv_sem=recv_sem.at[d, w],
            device_id=(plane(d + 1), y, z), device_id_type=MESH,
        )

    def rad_copy(d):
        return pltpu.make_async_remote_copy(
            src_ref=rad, dst_ref=far_rad.at[d], send_sem=rad_send.at[d], recv_sem=rad_recv.at[d],
            device_id=(plane(d + 1), y, z), device_id_type=MESH,
        )

    for d in range(2):
        rad_copy(d).start()
    for w in range(WIN):
        for d in range(2):
            coef_copy(w, d).start()

    for copy in loads:
        copy.wait()

    def prepare(w, carry):
        c = own[w]
        mu = jnp.mean(c, axis=1, keepdims=True)
        mean[w] = jnp.broadcast_to(mu, c.shape)
        feats = features(positions(basis, c - mu), True)
        for b in range(SAMP // SUB):
            lhs[w, b] = stacked(feats, b).T.astype(bf16)
        return carry

    lax.fori_loop(0, WIN, prepare, 0)
    pl.semaphore_wait(known.at[0], 2)
    tell(1, next_z)

    for d in range(2):
        rad_copy(d).wait_recv()
    column = jnp.broadcast_to(own_rad[...], (TILE, TILE)).T
    for d in range(2):
        scale[:, TILE * d : TILE * d + TILE] = -LOG2E / (column + far_rad[d])
    acc[...] = jnp.zeros_like(acc)

    rows = 32
    turn = lax.broadcasted_iota(jnp.int32, (rows, FEATS * SUB), 1) % SUB

    def window(w, carry):
        for d in range(2):
            coef_copy(w, d).wait_recv()
        mu = mean[w]
        c = jnp.concatenate([far[0, w] - mu, far[1, w] - mu], axis=1)
        feats = features(positions(basis, c), False)
        for b in range(SAMP // SUB):
            rhs = stacked(feats, b).astype(bf16)
            for i in range(TILE // rows):
                here = slice(rows * i, rows * i + rows)
                left = lhs[w, b, here, :]
                zero = jnp.zeros_like(left)
                big = jnp.concatenate([jnp.where(turn == s, left, zero) for s in range(SUB)], axis=0)
                dist = jnp.dot(big, rhs, preferred_element_type=f32)
                sc = scale[here, :]
                total = None
                for s in range(SUB):
                    term = jnp.exp2(dist[rows * s : rows * s + rows] * sc)
                    total = term if total is None else total + term
                acc[here, :] += total

        @pl.when(w == 0)
        def _():
            pl.semaphore_wait(known.at[1], 2)
            tell(2, next_plane)

        return carry

    lax.fori_loop(0, WIN, window, 0)

    sums = acc[...]
    part_r[0:1, :] = jnp.sum(sums[:, :TILE].T, axis=0, keepdims=True)
    part_r[1:2, :] = jnp.sum(sums[:, TILE:].T, axis=0, keepdims=True)
    column_sums = jnp.sum(sums, axis=0, keepdims=True)
    for d in range(2):
        part_c[d] = column_sums[:, TILE * d : TILE * d + TILE]

    def row_copy(a, k, ys, zs):
        slot = 4 * ys + zs
        return pltpu.make_async_remote_copy(
            src_ref=part_r, dst_ref=all_r.at[slot], send_sem=r_send.at[a, k], recv_sem=r_recv.at[slot],
            device_id=(g, other(y, a), other(z, k)), device_id_type=MESH,
        )

    def column_copy(d, a, k, ys, zs):
        slot = 4 * ys + zs
        return pltpu.make_async_remote_copy(
            src_ref=part_c.at[d], dst_ref=all_c.at[d, slot], send_sem=c_send.at[d, a, k], recv_sem=c_recv.at[d, slot],
            device_id=(plane(-d - 1), other(y, a), other(z, k)), device_id_type=MESH,
        )

    pl.semaphore_wait(known.at[2], 2)
    for a, k in FAR_FIRST:
        for d in range(2):
            column_copy(d, a, k, y, z).start()
        if a or k:
            row_copy(a, k, y, z).start()
    all_r[4 * y + z] = part_r[...]

    for d in range(2):
        rad_copy(d).wait_send()
        for w in range(WIN):
            coef_copy(w, d).wait_send()
    for a, k in reversed(FAR_FIRST):
        for d in range(2):
            column_copy(d, a, k, y, z).wait_send()
        if a or k:
            row_copy(a, k, y, z).wait_send()

    for a, k in reversed(FAR_FIRST):
        if a or k:
            row_copy(a, k, other(y, a), other(z, k)).wait_recv()
        for d in range(2):
            column_copy(d, a, k, other(y, a), other(z, k)).wait_recv()
    rows_total = jnp.sum(all_r[...], axis=0)
    for d in range(2):
        for r, line in ((2 * d, rows_total[d : d + 1, :]), (2 * d + 1, jnp.sum(all_c[d], axis=0))):
            out[r : r + 1, :] = jnp.where(own_mask[0, r] > 0, line, jnp.zeros_like(line))


def local(coeffs, radius, tile_mask):
    vmem = pltpu.VMEM
    dma = pltpu.SemaphoreType.DMA
    sums = pl.pallas_call(
        kernel,
        out_shape=jax.ShapeDtypeStruct((4, TILE), f32),
        in_specs=[pl.BlockSpec(memory_space=pltpu.HBM)] * 3,
        out_specs=pl.BlockSpec(memory_space=pltpu.VMEM),
        scratch_shapes=[
            vmem((WIN, 3 * K, TILE), f32),
            vmem((1, TILE), f32),
            pltpu.SMEM((1, ROUNDS), jnp.int32),
            vmem((2, WIN, 3 * K, TILE), f32),
            vmem((2, 1, TILE), f32),
            vmem((WIN, SAMP // SUB, TILE, FEATS * SUB), bf16),
            vmem((WIN, 3 * K, TILE), f32),
            vmem((TILE, 2 * TILE), f32),
            vmem((TILE, 2 * TILE), f32),
            vmem((2, TILE), f32),
            vmem((2, 1, TILE), f32),
            vmem((16, 2, TILE), f32),
            vmem((2, 16, 1, TILE), f32),
            dma((3,)),
            dma((2, WIN)),
            dma((2, WIN)),
            dma((2,)),
            dma((2,)),
            dma((4, 4)),
            dma((16,)),
            dma((2, 4, 4)),
            dma((2, 16)),
            pltpu.SemaphoreType.REGULAR((3,)),
        ],
        compiler_params=pltpu.CompilerParams(
            collective_id=0, has_side_effects=True, vmem_limit_bytes=32 << 20
        ),
    )(*[pltpu.with_memory_space_constraint(x, pltpu.HBM) for x in (coeffs.reshape(WIN, 3 * K, TILE), radius.reshape(1, TILE), tile_mask.reshape(1, ROUNDS))])
    time_count = lax.axis_size(TM)
    normalizer = 1.0 / (coeffs.shape[0] * time_count * SAMP * TILE)
    return sums * normalizer


def solution(mesh):
    torus = Mesh(mesh.devices.reshape(mesh.shape["plane"], 4, 4), ("plane", "tm_0", "tm_1"))
    in_specs = (P(TM, None, None, "plane"), P("plane"), P(None, "plane", None))
    out_specs = P(None, "plane")
    return jax.shard_map(local, mesh=torus, in_specs=in_specs, out_specs=out_specs, check_vma=False)
```

```python
import jax
import jax.numpy as jnp
from jax import lax
from jax.experimental import pallas as pl
from jax.experimental.pallas import tpu as pltpu
from jax.sharding import Mesh
from jax.sharding import PartitionSpec as P

SAMP = 32
TILE = 128
ROUNDS = 4
K = 16
WIN = 4
FEATS = 24
SUB = 8
LOG2E = 1.4426950408889634
TM = ("tm_0", "tm_1")
FAR_FIRST = sorted(
    ((a, k) for a in range(4) for k in range(4)), key=lambda s: -(min(s[0], 4 - s[0]) + 2 * min(s[1], 4 - s[1]))
)
MESH = pl.DeviceIdType.MESH
f32 = jnp.float32
bf16 = jnp.bfloat16


def split3(x):
    h = x.astype(bf16).astype(f32)
    rest = x - h
    m = rest.astype(bf16).astype(f32)
    return h, m, rest - m


def basis_parts():
    shape = (SAMP, 5 * K)
    sample = lax.broadcasted_iota(jnp.int32, shape, 0).astype(f32)
    lane = lax.broadcasted_iota(jnp.int32, shape, 1)
    degree = lane % K
    t = -1.0 + (2.0 * sample + 1.0) / SAMP
    before, now = jnp.ones_like(t), t
    table = jnp.where(degree == 0, before, now)
    for k in range(2, K):
        before, now = now, 2.0 * t * now - before
        table = jnp.where(degree == k, now, table)
    h, m, l = split3(table)
    part = lane // K
    return jnp.where(part == 4, l, jnp.where(part == 2, m, h)).astype(bf16)


def positions(basis, coef):
    n = coef.shape[1]
    h, m, l = split3(coef)
    columns = []
    for c in range(3):
        rows = slice(K * c, K * c + K)
        columns.append(jnp.concatenate([h[rows], m[rows], h[rows], l[rows], h[rows]], axis=0).astype(bf16))
    pos = jnp.dot(basis, jnp.concatenate(columns, axis=1), preferred_element_type=f32)
    return [pos[:, c * n : (c + 1) * n] for c in range(3)]


def features(pos, own):
    parts = [split3(p) for p in pos]
    norm = pos[0] * pos[0] + pos[1] * pos[1] + pos[2] * pos[2]
    norms = list(split3(norm))
    ones = [jnp.ones_like(norm)] * 3
    if own:
        return [-2.0 * parts[c][r] for r in (0, 0, 1, 0, 2, 1) for c in range(3)] + ones + norms
    return [parts[c][r] for r in (0, 1, 0, 2, 0, 1) for c in range(3)] + norms + ones


def stacked(feats, b):
    return jnp.concatenate([f[SUB * b : SUB * b + SUB] for f in feats], axis=0)


def kernel(
    coef, rad, mask, out,
    own, own_rad, own_mask, far, far_rad, lhs, mean, scale, acc, part_r, part_c, all_r, all_c,
    load_sem, send_sem, recv_sem, rad_send, rad_recv, r_send, r_recv, c_send, c_recv, known,
):
    planes = lax.axis_size("plane")
    g = lax.axis_index("plane")
    y = lax.axis_index("tm_0")
    z = lax.axis_index("tm_1")

    def plane(step):
        return lax.rem(g + step + planes, planes)

    def other(i, step):
        return lax.rem(i + step, 4)

    barrier = pltpu.get_barrier_semaphore()

    def greet(device):
        pl.semaphore_signal(barrier, inc=1, device_id=device, device_id_type=MESH)

    for d in (1, 2):
        greet((plane(-d), y, z))
    for k in (1, 3):
        greet((g, y, other(z, k)))
    for k in (2, 1, 3):
        greet((g, other(y, k), z))

    loads = [
        pltpu.make_async_copy(coef, own, load_sem.at[0]),
        pltpu.make_async_copy(rad, own_rad, load_sem.at[1]),
        pltpu.make_async_copy(mask, own_mask, load_sem.at[2]),
    ]
    for copy in loads:
        copy.start()
    basis = basis_parts()

    pl.semaphore_wait(barrier, 7)

    def tell(turn, devices):
        for device in devices:
            pl.semaphore_signal(known.at[turn], inc=1, device_id=device, device_id_type=MESH)

    next_z = [(g, y, other(z, k)) for k in (1, 3)]
    next_plane = [(plane(d), y, z) for d in (1, 2)]
    tell(0, next_z)

    def coef_copy(w, d):
        return pltpu.make_async_remote_copy(
            src_ref=own.at[w], dst_ref=far.at[d, w], send_sem=send_sem.at[d, w], recv_sem=recv_sem.at[d, w],
            device_id=(plane(d + 1), y, z), device_id_type=MESH,
        )

    def rad_copy(d):
        return pltpu.make_async_remote_copy(
            src_ref=own_rad, dst_ref=far_rad.at[d], send_sem=rad_send.at[d], recv_sem=rad_recv.at[d],
            device_id=(plane(d + 1), y, z), device_id_type=MESH,
        )

    for copy in loads:
        copy.wait()

    for d in range(2):
        rad_copy(d).start()
    for w in range(WIN):
        for d in range(2):
            coef_copy(w, d).start()

    def prepare(w, carry):
        c = own[w]
        mu = jnp.mean(c, axis=1, keepdims=True)
        mean[w] = jnp.broadcast_to(mu, c.shape)
        feats = features(positions(basis, c - mu), True)
        for b in range(SAMP // SUB):
            lhs[w, b] = stacked(feats, b).T.astype(bf16)
        return carry

    lax.fori_loop(0, WIN, prepare, 0)
    pl.semaphore_wait(known.at[0], 2)
    tell(1, next_z)

    for d in range(2):
        rad_copy(d).wait_recv()
    column = jnp.broadcast_to(own_rad[...], (TILE, TILE)).T
    for d in range(2):
        scale[:, TILE * d : TILE * d + TILE] = -LOG2E / (column + far_rad[d])
    acc[...] = jnp.zeros_like(acc)

    rows = 32
    turn = lax.broadcasted_iota(jnp.int32, (rows, FEATS * SUB), 1) % SUB

    def window(w, carry):
        for d in range(2):
            coef_copy(w, d).wait_recv()
        mu = mean[w]
        c = jnp.concatenate([far[0, w] - mu, far[1, w] - mu], axis=1)
        feats = features(positions(basis, c), False)
        for b in range(SAMP // SUB):
            rhs = stacked(feats, b).astype(bf16)
            for i in range(TILE // rows):
                here = slice(rows * i, rows * i + rows)
                left = lhs[w, b, here, :]
                zero = jnp.zeros_like(left)
                big = jnp.concatenate([jnp.where(turn == s, left, zero) for s in range(SUB)], axis=0)
                dist = jnp.dot(big, rhs, preferred_element_type=f32)
                sc = scale[here, :]
                total = None
                for s in range(SUB):
                    term = jnp.exp2(dist[rows * s : rows * s + rows] * sc)
                    total = term if total is None else total + term
                acc[here, :] += total

        @pl.when(w == 0)
        def _():
            pl.semaphore_wait(known.at[1], 2)
            tell(2, next_plane)

        return carry

    lax.fori_loop(0, WIN, window, 0)

    sums = acc[...]
    part_r[0:1, :] = jnp.sum(sums[:, :TILE].T, axis=0, keepdims=True)
    part_r[1:2, :] = jnp.sum(sums[:, TILE:].T, axis=0, keepdims=True)
    column_sums = jnp.sum(sums, axis=0, keepdims=True)
    for d in range(2):
        part_c[d] = column_sums[:, TILE * d : TILE * d + TILE]

    def row_copy(a, k, ys, zs):
        slot = 4 * ys + zs
        return pltpu.make_async_remote_copy(
            src_ref=part_r, dst_ref=all_r.at[slot], send_sem=r_send.at[a, k], recv_sem=r_recv.at[slot],
            device_id=(g, other(y, a), other(z, k)), device_id_type=MESH,
        )

    def column_copy(d, a, k, ys, zs):
        slot = 4 * ys + zs
        return pltpu.make_async_remote_copy(
            src_ref=part_c.at[d], dst_ref=all_c.at[d, slot], send_sem=c_send.at[d, a, k], recv_sem=c_recv.at[d, slot],
            device_id=(plane(-d - 1), other(y, a), other(z, k)), device_id_type=MESH,
        )

    pl.semaphore_wait(known.at[2], 2)
    for a, k in FAR_FIRST:
        for d in range(2):
            column_copy(d, a, k, y, z).start()
        if a or k:
            row_copy(a, k, y, z).start()
    all_r[4 * y + z] = part_r[...]

    for d in range(2):
        rad_copy(d).wait_send()
        for w in range(WIN):
            coef_copy(w, d).wait_send()
    for a, k in reversed(FAR_FIRST):
        for d in range(2):
            column_copy(d, a, k, y, z).wait_send()
        if a or k:
            row_copy(a, k, y, z).wait_send()

    for a, k in reversed(FAR_FIRST):
        if a or k:
            row_copy(a, k, other(y, a), other(z, k)).wait_recv()
        for d in range(2):
            column_copy(d, a, k, other(y, a), other(z, k)).wait_recv()
    rows_total = jnp.sum(all_r[...], axis=0)
    for d in range(2):
        for r, line in ((2 * d, rows_total[d : d + 1, :]), (2 * d + 1, jnp.sum(all_c[d], axis=0))):
            out[r : r + 1, :] = jnp.where(own_mask[0, r] > 0, line, jnp.zeros_like(line))


def local(coeffs, radius, tile_mask):
    vmem = pltpu.VMEM
    dma = pltpu.SemaphoreType.DMA
    sums = pl.pallas_call(
        kernel,
        out_shape=jax.ShapeDtypeStruct((4, TILE), f32),
        in_specs=[pl.BlockSpec(memory_space=pltpu.HBM)] * 3,
        out_specs=pl.BlockSpec(memory_space=pltpu.VMEM),
        scratch_shapes=[
            vmem((WIN, 3 * K, TILE), f32),
            vmem((1, TILE), f32),
            pltpu.SMEM((1, ROUNDS), jnp.int32),
            vmem((2, WIN, 3 * K, TILE), f32),
            vmem((2, 1, TILE), f32),
            vmem((WIN, SAMP // SUB, TILE, FEATS * SUB), bf16),
            vmem((WIN, 3 * K, TILE), f32),
            vmem((TILE, 2 * TILE), f32),
            vmem((TILE, 2 * TILE), f32),
            vmem((2, TILE), f32),
            vmem((2, 1, TILE), f32),
            vmem((16, 2, TILE), f32),
            vmem((2, 16, 1, TILE), f32),
            dma((3,)),
            dma((2, WIN)),
            dma((2, WIN)),
            dma((2,)),
            dma((2,)),
            dma((4, 4)),
            dma((16,)),
            dma((2, 4, 4)),
            dma((2, 16)),
            pltpu.SemaphoreType.REGULAR((3,)),
        ],
        compiler_params=pltpu.CompilerParams(
            collective_id=0, has_side_effects=True, vmem_limit_bytes=32 << 20
        ),
    )(*[pltpu.with_memory_space_constraint(x, pltpu.HBM) for x in (coeffs.reshape(WIN, 3 * K, TILE), radius.reshape(1, TILE), tile_mask.reshape(1, ROUNDS))])
    time_count = lax.axis_size(TM)
    normalizer = 1.0 / (coeffs.shape[0] * time_count * SAMP * TILE)
    return sums * normalizer


def solution(mesh):
    torus = Mesh(mesh.devices.reshape(mesh.shape["plane"], 4, 4), ("plane", "tm_0", "tm_1"))
    in_specs = (P(TM, None, None, "plane"), P("plane"), P(None, "plane", None))
    out_specs = P(None, "plane")
    return jax.shard_map(local, mesh=torus, in_specs=in_specs, out_specs=out_specs, check_vma=False)
```
